256 devices in a mesh: replica: 4 (over y_lo, core), fsdp: 8 (over z), tensor: 8 (over x, y_hi).
Axes of the slice: x: 4, y: 4 (y_hi: 2, y_lo: 2; y = y_hi * 2 + y_lo), z: 8, core: 2. Of those that a mesh axis runs over, the one named last changes fastest.
Arguments:
- tokens: bfloat16 [16384, 8192], P(('replica', 'fsdp')), may hold values from -6 to 6
- norm_gain: float32 [8192], replicated, may hold values from 0.1 to 1.9
- outer_base: float32 [2, 8192, 1024], P(None, 'fsdp', 'tensor'), may hold values from -0.0625 to 0.0625
- momentum: float32 [2, 8192, 1024], P(None, 'fsdp', 'tensor'), may hold values from -0.06 to 0.06
- inner_params: bfloat16 [4, 2, 8192, 1024], P('replica', None, 'fsdp', 'tensor'), may hold values from -0.0625 to 0.0625
Outputs:
- new_base: float32 [2, 8192, 1024], P(None, ('fsdp', 'replica'), 'tensor')
- new_momentum: float32 [2, 8192, 1024], P(None, ('fsdp', 'replica'), 'tensor')
- keys: bfloat16 [16384, 1024], P(('replica', 'fsdp'), 'tensor')
- values: bfloat16 [16384, 1024], P(('replica', 'fsdp'), 'tensor')
The draws below stay inside these ranges and needn't reach their ends.
All inputs are finite; a program needn't handle non-finite values.
Results may differ from the reference program's by a relative error of at most 0.018.
Values may be sent and summed in bfloat16 or wider, within the bound.
No kernel may reach another device: no remote copies, remote signals or barrier semaphores. Data moves between devices by JAX's collectives and lax.ppermute only.
A program may use at most 64 MiB of HBM per device.

```python
import jax
import jax.numpy as jnp
from jax import lax

D = 8192
KV = 1024
TOKENS = 16384
N_REPLICA = 4


def levels(own_key, shape, split, smallest, top_value):
    level = 1.0
    for dim, blocks in split:
        heights = jax.random.uniform(jax.random.fold_in(jax.random.fold_in(own_key, 6), dim), (blocks,), jnp.float32, smallest / len(split), top_value / len(split))
        level = level * jnp.repeat(jnp.exp(heights), shape[dim] // blocks).reshape((-1,) + (1,) * (len(shape) - 1 - dim))
    return level


def normal_values(stream_key, extent, width, bound, cuts=(), kind=jnp.bfloat16):
    array = jax.random.normal(stream_key, extent, jnp.float32) * width
    if len(cuts) > 0:
        array = levels(stream_key, extent, cuts, -0.22, 0.18) * array
    return jnp.clip(array, min=-bound, max=bound).astype(kind)


def setup_inputs(seed: int = 0) -> dict:
    streams_of = jax.random.split(jax.random.key(seed), 6)
    tokens = normal_values(streams_of[0], (TOKENS, D), 1.0, 6.0, ((0, 32),))
    norm_gain = jnp.clip(1.0 + 0.18 * jax.random.normal(streams_of[1], (D,), jnp.float32), 0.1, 1.9)
    outer_base = normal_values(streams_of[2], (2, D, KV), D ** -0.5, 0.0625, ((1, 8), (2, 8)), jnp.float32)
    momentum = normal_values(streams_of[3], (2, D, KV), 0.01, 0.06, ((1, 8), (2, 8)), jnp.float32)
    inner_params = normal_values(streams_of[4], (N_REPLICA, 2, D, KV), D ** -0.5, 0.0625, ((0, 4), (2, 8), (3, 8)))
    return dict(tokens=tokens, norm_gain=norm_gain, outer_base=outer_base, momentum=momentum, inner_params=inner_params)


momentum_rate = 0.9
outer_rate = 0.7
epsilon = 1e-05

def reference(tokens, norm_gain, outer_base, momentum, inner_params):
    deltas = (outer_base[None] - inner_params.astype(jnp.float32)).astype(jnp.bfloat16)
    average = lax.optimization_barrier(jnp.sum(deltas.astype(jnp.float32), axis=0)) / N_REPLICA
    new_momentum = momentum_rate * momentum + average
    new_base = outer_base - outer_rate * (average + momentum_rate * new_momentum)
    weights = new_base.astype(jnp.bfloat16)
    inputs = tokens.astype(jnp.float32)
    scale = lax.rsqrt(lax.optimization_barrier(jnp.mean(inputs * inputs, axis=-1, keepdims=True)) + epsilon)
    normed = (inputs * scale * norm_gain).astype(jnp.bfloat16)
    keys = jnp.dot(normed, weights[0], preferred_element_type=jnp.float32).astype(jnp.bfloat16)
    values = jnp.dot(normed, weights[1], preferred_element_type=jnp.float32).astype(jnp.bfloat16)
    return (new_base, new_momentum, keys, values)
```

```python
import functools

import jax
import jax.numpy as jnp
from jax import lax
from jax.experimental import pallas as pl
from jax.experimental.pallas import tpu as pltpu
from jax.sharding import PartitionSpec as P

momentum_rate = 0.9
outer_rate = 0.7
epsilon = 1e-05


F32, BF16 = jnp.float32, jnp.bfloat16
ON_CHIP = [(r, r ^ 1) for r in range(4)]
ACROSS = [(r, r ^ 2) for r in range(4)]


def ring(step, size):
    return [(z, (z + step) % size) for z in range(size)]


def nesterov(base, momentum, average):
    new_momentum = momentum_rate * momentum + average
    new_base = base - outer_rate * (average + momentum_rate * new_momentum)
    return new_base, new_momentum


def pack_kernel(where, x_ref, keep_ref, send_ref, scale_ref):
    y, c = where[1], where[2]
    step = pl.program_id(0)
    for other in range(2):
        row = y + other - 2 * other * y
        for ref, core in ((keep_ref, c), (send_ref, 1 - c)):
            at = pl.multiple_of(256 * (2 * row + core), 256)
            ref[0, :, 128 * other : 128 * other + 128] = x_ref[:, pl.ds(at, 128)]
            at = pl.multiple_of(at + 128, 128)
            ref[0, :, 256 + 128 * other : 384 + 128 * other] = x_ref[:, pl.ds(at, 128)]

    @pl.when(step == 0)
    def _():
        scale_ref[...] = jnp.zeros_like(scale_ref)

    for top in range(0, x_ref.shape[0], 64):
        total = scale_ref[top : top + 64, :]
        for left in range(0, x_ref.shape[1], 128):
            piece = x_ref[top : top + 64, left : left + 128].astype(F32)
            total = total + piece * piece
        scale_ref[top : top + 64, :] = total

    @pl.when(step == pl.num_programs(0) - 1)
    def _():
        features = x_ref.shape[1] * pl.num_programs(0)
        mean = jnp.sum(scale_ref[...], axis=1, keepdims=True) / features
        scale_ref[...] = jnp.broadcast_to(lax.rsqrt(mean + epsilon), scale_ref.shape)


def pack(tokens, where, shards):
    rows, features = tokens.shape
    wide = features // shards
    half = jax.ShapeDtypeStruct((shards, rows, wide // 2), BF16)
    out = pl.BlockSpec((1, rows, wide // 2), lambda s, w: (s, 0, 0))
    return pl.pallas_call(
        pack_kernel,
        grid_spec=pltpu.PrefetchScalarGridSpec(
            num_scalar_prefetch=1,
            grid=(shards,),
            in_specs=[pl.BlockSpec((rows, wide), lambda s, w: (0, lax.rem(w[0] + s, shards)))],
            out_specs=[out, out, pl.BlockSpec((rows, 128), lambda s, w: (0, 0))],
        ),
        out_shape=[half, half, jax.ShapeDtypeStruct((rows, 128), F32)],
        cost_estimate=pl.CostEstimate(flops=rows * features * 3, bytes_accessed=rows * features * 4, transcendentals=0),
        name="pack",
    )(where, tokens)


def side(ref, *at):
    return jnp.concatenate([ref[(*at, 0)], ref[(*at, 1)]], axis=1)


def mm_kernel(sets, hops, has_acc, cast, *refs):
    xs, rest = refs[: sets * hops], refs[sets * hops :]
    ws, rest = rest[: 3 * hops], rest[3 * hops :]
    accs, outs = rest[:-sets], rest[-sets:]
    rhs = [
        jnp.concatenate([side(a), side(o), side(b, 0), side(b, 1)], axis=0)
        for a, o, b in (ws[3 * h : 3 * h + 3] for h in range(hops))
    ]
    for n in range(sets):
        total = accs[n][...] if has_acc else None
        for h in range(hops):
            term = jnp.dot(xs[n * hops + h][0], rhs[h], preferred_element_type=F32)
            total = term if total is None else total + term
        outs[n][...] = total.astype(outs[n].dtype)


def multiply(xs, hops, weights, accs, dtype=F32, name="mm"):
    rows, deep = xs[0].shape[1:]
    whole = pl.BlockSpec(memory_space=pltpu.VMEM)
    args, specs = [], []
    for x in xs:
        for hop in hops:
            args.append(x)
            specs.append(pl.BlockSpec((1, rows, deep), lambda i, hop=hop: (hop, 0, 0)))
    for w in weights:
        args.extend(w)
        for piece in w:
            specs.append(pl.BlockSpec(piece.shape, lambda i, n=piece.ndim: (0,) * n))
    out = pl.BlockSpec((rows, 256), lambda i: (0, 0))
    if accs is not None:
        args.extend(accs)
        specs.extend([out] * len(accs))
    return pl.pallas_call(
        functools.partial(mm_kernel, len(xs), len(hops), accs is not None, dtype),
        grid=(1,),
        in_specs=specs,
        out_specs=[out] * len(xs),
        out_shape=[jax.ShapeDtypeStruct((rows, 256), dtype)] * len(xs),
        cost_estimate=pl.CostEstimate(
            flops=2 * rows * deep * 256 * len(xs) * len(hops),
            bytes_accessed=2 * rows * deep * len(xs) * len(hops),
            transcendentals=0,
        ),
        name=name,
    )(*args)


def on_device(tokens, norm_gain, outer_base, momentum, inner_params):
    shards = lax.axis_size("fsdp")
    z, r = lax.axis_index("fsdp"), lax.axis_index("replica")
    y, c = r // 2, r % 2
    up, down = ring(1, shards), ring(-1, shards)

    def hop(x, perm, axis="fsdp"):
        return lax.ppermute(x, axis, perm)

    def split(x):
        return x.reshape(2, 2, 2, 2, 128, 128)

    def of_core(x, core):
        return lax.dynamic_index_in_dim(x, core, 2, keepdims=False)

    def of_chip(x, chip):
        return lax.dynamic_index_in_dim(x, chip, 1, keepdims=False)

    base, mom, inner = split(outer_base), split(momentum), split(inner_params[0])

    def delta(core):
        return (of_core(base, core) - of_core(inner, core).astype(F32)).astype(BF16)

    sent = lax.optimization_barrier(delta(1 - c))
    from_core = hop(sent, ON_CHIP, "replica")
    kept = delta(c)
    pair = (kept.astype(F32) + from_core.astype(F32)).astype(BF16)
    own, other = of_chip(pair, y), of_chip(pair, 1 - y)
    a_sent = other[:, 0]
    b_sent = jnp.stack([other[:, 1], own[:, 1]])
    a_got = hop(a_sent, ACROSS, "replica")
    b_got = hop(b_sent, ACROSS, "replica")

    gains = norm_gain.reshape(shards, 2, 2, 2, 128)
    gain = lax.dynamic_index_in_dim(lax.dynamic_index_in_dim(gains, z, 0, False), c, 1, False)
    gain = jnp.broadcast_to(gain[..., None], (2, 2, 128, 128))
    gain_own = lax.dynamic_index_in_dim(gain, y, 0, False)
    gain_other = lax.dynamic_index_in_dim(gain, 1 - y, 0, False)
    base_c, mom_c = of_core(base, c), of_core(mom, c)
    base_own, base_other = of_chip(base_c, y), of_chip(base_c, 1 - y)
    mom_own, mom_other = of_chip(mom_c, y), of_chip(mom_c, 1 - y)

    def update(mine, got, base, mom, gain):
        average = (mine.astype(F32) + got.astype(F32)) / 4
        new_base, new_mom = nesterov(base, mom, average)
        return new_base, new_mom, (new_base * gain).astype(BF16)

    base_a, mom_a, weight_a = update(own[:, 0], a_got, base_own[:, 0], mom_own[:, 0], gain_own[0])
    base_b, mom_b, weight_b0 = update(own[:, 1], b_got[0], base_own[:, 1], mom_own[:, 1], gain_own[1])
    _, _, weight_b1 = update(other[:, 1], b_got[1], base_other[:, 1], mom_other[:, 1], gain_other[1])
    new_base = jnp.concatenate([base_a, base_b], axis=1)
    new_mom = jnp.concatenate([mom_a, mom_b], axis=1)
    weight_b = jnp.stack([weight_b0, weight_b1])

    where = jnp.stack([z, y, c]).astype(jnp.int32)
    mine, theirs, scale = pack(tokens, where, shards)
    theirs = hop(theirs, ON_CHIP, "replica")

    ups, downs = [(weight_a, weight_b)], [(weight_a, weight_b)]
    crossed = [hop(weight_a, ACROSS, "replica")]
    crossed_up, crossed_down = crossed[:], crossed[:]
    half = shards // 2
    for _ in range(1, half):
        a_up, a_down = hop(ups[-1][0], up), hop(downs[-1][0], down)
        b_up, b_down = hop(ups[-1][1], up), hop(downs[-1][1], down)
        ups.append((a_up, b_up))
        downs.append((a_down, b_down))
        crossed_up.append(hop(a_up, ACROSS, "replica"))
        crossed_down.append(hop(a_down, ACROSS, "replica"))
    far = (hop(ups[-1][0], up), hop(crossed_up[-1], up), hop(downs[-1][1], down))

    accs = multiply([mine, theirs], [0], [(weight_a, crossed[0], weight_b)], None, name="mm0")
    for n in range(1, half):
        accs = multiply(
            [mine, theirs],
            [shards - n, n],
            [(ups[n][0], crossed_up[n], ups[n][1]), (downs[n][0], crossed_down[n], downs[n][1])],
            accs,
            name=f"mm{n}",
        )
    (part,) = multiply([theirs], [half], [far], accs[1:], BF16, name="mm_theirs")
    part = hop(part, ON_CHIP, "replica")
    (total,) = multiply([mine], [half], [far], accs[:1], name="mm_mine")
    total = (total + part.astype(F32)) * scale[:, :1]
    return new_base.reshape(2, 256, 128), new_mom.reshape(2, 256, 128), total[:, :128].astype(BF16), total[:, 128:].astype(BF16)


def solution(mesh):
    placed = (
        P(("replica", "fsdp"), None),
        P(),
        P(None, "fsdp", "tensor"),
        P(None, "fsdp", "tensor"),
        P("replica", None, "fsdp", "tensor"),
    )
    return jax.shard_map(
        on_device,
        mesh=mesh,
        in_specs=placed,
        out_specs=(
            P(None, ("fsdp", "replica"), "tensor"),
            P(None, ("fsdp", "replica"), "tensor"),
            P(("replica", "fsdp"), "tensor"),
            P(("replica", "fsdp"), "tensor"),
        ),
        check_vma=False,
    )
```

```python
import functools

import jax
import jax.numpy as jnp
from jax import lax
from jax.experimental import pallas as pl
from jax.experimental.pallas import tpu as pltpu
from jax.sharding import PartitionSpec as P

momentum_rate = 0.9
outer_rate = 0.7
epsilon = 1e-05


F32, BF16 = jnp.float32, jnp.bfloat16
IN_HBM = pl.BlockSpec(memory_space=pltpu.HBM)
IN_VMEM = pl.BlockSpec(memory_space=pltpu.VMEM)
GRANT = 16 * 1024 * 1024
ON_CHIP = [(r, r ^ 1) for r in range(4)]
ACROSS = [(r, r ^ 2) for r in range(4)]


def ring(size):
    return [(r * size + z, r * size + (z + 1 - 2 * (r % 2)) % size) for r in range(4) for z in range(size)]


def position():
    r = lax.axis_index("replica")
    return lax.div(r, 2), lax.rem(r, 2)


def quarter(q, y, core):
    return 2 * (1 - y if q else y) + core


def call(kernel, args, out, scratch=(), flops=0, moved=0, name=None):
    spaces = [s for _, s in args]
    return pl.pallas_call(
        kernel,
        in_specs=[IN_HBM if s is pltpu.HBM else IN_VMEM for s in spaces],
        out_specs=[IN_VMEM] * len(out),
        out_shape=out,
        scratch_shapes=list(scratch),
        compiler_params=pltpu.CompilerParams(vmem_limit_bytes=GRANT),
        cost_estimate=pl.CostEstimate(flops=flops, bytes_accessed=moved, transcendentals=0),
        name=name,
    )(*[pltpu.with_memory_space_constraint(a, s) for a, s in args])


def sent_kernel(base_hbm, inner_hbm, out_ref, base, inner, sems):
    y, core = position()
    copies = []
    for n in range(4):
        at = quarter(n // 2, y, 1 - core)
        copies.append(pltpu.make_async_copy(base_hbm.at[n % 2, at], base.at[n], sems.at[0, n]))
        copies.append(pltpu.make_async_copy(inner_hbm.at[n % 2, at], inner.at[n], sems.at[1, n]))
    for copy in copies:
        copy.start()
    for n in range(4):
        copies[2 * n].wait()
        copies[2 * n + 1].wait()
        out_ref[n // 2, n % 2] = (base[n] - inner[n].astype(F32)).astype(BF16)


def kept_kernel(base_hbm, inner_hbm, mom_hbm, out_ref, base_ref, mom_ref, inner, sems):
    y, core = position()
    copies, later = [], []
    for n in range(4):
        at, to = quarter(n // 2, y, core), (n // 2, n % 2)
        copies.append(pltpu.make_async_copy(base_hbm.at[n % 2, at], base_ref.at[to], sems.at[0, n]))
        copies.append(pltpu.make_async_copy(inner_hbm.at[n % 2, at], inner.at[n], sems.at[1, n]))
        later.append(pltpu.make_async_copy(mom_hbm.at[n % 2, at], mom_ref.at[to], sems.at[2, n]))
    for copy in copies + later:
        copy.start()
    for n in range(4):
        copies[2 * n].wait()
        copies[2 * n + 1].wait()
        out_ref[n // 2, n % 2] = (base_ref[n // 2, n % 2] - inner[n].astype(F32)).astype(BF16)
    for copy in later:
        copy.wait()


def pair_kernel(kept_ref, got_ref, first_ref, second_ref):
    first_ref[...] = (kept_ref[0].astype(F32) + got_ref[0].astype(F32)).astype(BF16)
    second_ref[...] = (kept_ref[1].astype(F32) + got_ref[1].astype(F32)).astype(BF16)


def update_kernel(place, pair_ref, got_ref, base_ref, mom_ref, block_ref, *out):
    for k in range(2):
        average = (pair_ref[k].astype(F32) + got_ref[k].astype(F32)) / 4
        new_mom = momentum_rate * mom_ref[place, k] + average
        new_base = base_ref[place, k] - outer_rate * (average + momentum_rate * new_mom)
        block_ref[:, 128 * k : 128 * k + 128] = new_base.astype(BF16)
        if out:
            out[0][k], out[1][k] = new_base, new_mom


def stage_kernel(hops, x_hbm, gain_ref, out_ref, sum_ref, sems):
    y, core = position()
    size = lax.axis_size("fsdp")
    z = lax.axis_index("fsdp")
    copies, rows = [], []
    for n, hop in enumerate(hops):
        source = lax.rem(z + hop * (2 * core - 1) + size, size)
        for q in range(4):
            at = 4 * source + quarter(q % 2, y, core if q < 2 else 1 - core)
            columns = pl.ds(pl.multiple_of(256 * at, 256), 256)
            copies.append(
                pltpu.make_async_copy(
                    x_hbm.at[:, columns], out_ref.at[n, :, 256 * q : 256 * q + 256], sems.at[n, q]
                )
            )
            rows.append(at)
    for copy in copies:
        copy.start()
    sum_ref[...] = jnp.zeros_like(sum_ref)
    for n in range(len(hops)):
        gains = []
        for q in range(4):
            copies[4 * n + q].wait()
            gains.append(gain_ref[pl.ds(rows[4 * n + q], 1), :])

        @pl.loop(0, x_hbm.shape[0] // 32)
        def _(step):
            tops = pl.ds(pl.multiple_of(32 * step, 32), 32)
            total = sum_ref[tops, :]
            for q in range(4):
                for left in range(0, 256, 128):
                    lanes = slice(256 * q + left, 256 * q + left + 128)
                    piece = out_ref[n, tops, lanes].astype(F32)
                    total = total + piece * piece
                    out_ref[n, tops, lanes] = (piece * gains[q][:, left : left + 128]).astype(BF16)
            sum_ref[tops, :] = total


def product(terms, staged, acc, sums, features, name):
    xs = list({id(staged[hop][0]): staged[hop][0] for hop, _, _ in terms}.values())
    args = [*xs]
    plan = []
    for hop, swapped, halves in terms:
        array, at = staged[hop]
        plan.append(([id(x) for x in xs].index(id(array)), at, swapped, len(args)))
        args.extend(halves)
    rows = xs[0].shape[1]
    if acc is not None:
        args.append(acc)
    if sums is not None:
        args.extend(sums)
    end = len(args)

    def kernel(*refs):
        total = None if acc is None else refs[end - 1 - (len(sums) if sums else 0)][...]
        for array, at, swapped, w in plan:
            for h in range(2):
                side = (1 - h if swapped else h) * 512
                term = jnp.dot(refs[array][at, :, side : side + 512], refs[w + h][...], preferred_element_type=F32)
                total = term if total is None else total + term
        if sums is None:
            refs[end][...] = total
            return
        squares = sum(refs[end - 1 - n][...] for n in range(len(sums)))
        total = total * lax.rsqrt(jnp.sum(squares, axis=1, keepdims=True) / features + epsilon)
        refs[end][...] = total[:, :128].astype(BF16)
        refs[end + 1][...] = total[:, 128:].astype(BF16)

    if sums is None:
        out = [pltpu.VMEM((rows, 256), F32)]
    else:
        out = [jax.ShapeDtypeStruct((rows, 128), BF16)] * 2
    return call(
        kernel,
        [(a, pltpu.VMEM) for a in args],
        out,
        flops=2 * rows * 1024 * 256 * len(terms),
        moved=rows * 2048 * len(terms),
        name=name,
    )


def on_device(tokens, norm_gain, outer_base, momentum, inner_params):
    shards = lax.axis_size("fsdp")
    way = ring(shards)
    HBM, VMEM = pltpu.HBM, pltpu.VMEM

    def hop(x):
        return lax.ppermute(x, ("replica", "fsdp"), way)

    def swap(x):
        return lax.ppermute(x, "replica", ON_CHIP)

    def across(x):
        return lax.ppermute(x, "replica", ACROSS)

    def tie(*xs):
        return lax.optimization_barrier(xs)

    base = outer_base.reshape(2, 4, 256, 128)
    mom = momentum.reshape(2, 4, 256, 128)
    inner = inner_params.reshape(2, 4, 256, 128)
    rows, features = tokens.shape
    gains = norm_gain.reshape(4 * shards, 256)
    half_shape = (2, 2, 256, 128)

    (sent,) = call(
        sent_kernel,
        [(base, HBM), (inner, HBM)],
        [VMEM(half_shape, BF16)],
        [VMEM((4, 256, 128), F32), VMEM((4, 256, 128), BF16), pltpu.SemaphoreType.DMA((2, 4))],
        name="sent",
    )
    from_core = swap(sent)
    kept, base_c, mom_c = call(
        kept_kernel,
        [(base, HBM), (inner, HBM), (mom, HBM)],
        [VMEM(half_shape, BF16), VMEM(half_shape, F32), VMEM(half_shape, F32)],
        [VMEM((4, 256, 128), BF16), pltpu.SemaphoreType.DMA((3, 4))],
        name="kept",
    )
    kept, from_core = tie(kept, from_core)
    pair = call(
        pair_kernel, [(kept, VMEM), (from_core, VMEM)], [VMEM((2, 256, 128), BF16)] * 2, name="pair"
    )
    got = [across(pair[1]), across(pair[0])]

    half = shards // 2
    staged, sums = {}, []

    def stage(hops, after, name):
        x, after = tie(gains, after)
        block, squares = call(
            functools.partial(stage_kernel, hops),
            [(tokens, HBM), (x, VMEM)],
            [VMEM((len(hops), rows, features // shards), BF16), VMEM((rows, 128), F32)],
            [pltpu.SemaphoreType.DMA((len(hops), 4))],
            flops=4 * rows * 1024 * len(hops),
            moved=rows * 2048 * len(hops),
            name=name,
        )
        for i, n in enumerate(hops):
            staged[n] = (block, i)
        sums.append(squares)
        return squares

    def update(place, mine, theirs):
        out = [VMEM((256, 256), BF16)]
        if place == 0:
            out += [VMEM((2, 256, 128), F32)] * 2
        args = [(mine, VMEM), (theirs, VMEM), (base_c, VMEM), (mom_c, VMEM)]
        return call(functools.partial(update_kernel, place), args, out, name=f"update{place}")

    done = stage([0, 1, -1], pair[0], "stage0")
    theirs, _ = tie(got[0], done)
    own, new_base, new_mom = update(0, pair[0], theirs)
    first = [hop(own)]
    done = stage([2, -2], own, "stage1")
    theirs, own, _ = tie(got[1], own, done)
    (second,) = update(1, pair[1], theirs)
    first.append(hop(second))

    mine = jnp.concatenate([own, second], axis=0)
    other = swap(mine)
    b = hop(other)
    mine, other = tie(mine, other)
    (acc,) = product([(0, False, [mine, other])], staged, None, None, features, "mm0")
    done = stage([3, -3, half], acc, "stage2")
    first[0], first[1], _ = tie(*first, done)
    a = jnp.concatenate(first, axis=0)
    held = None
    for n in range(1, half):
        next_a = hop(a)
        from_a = swap(a)
        if n + 1 < half:
            next_b = hop(b)
        from_b = swap(b)
        if held is not None:
            held, b = tie(held, b)
            (acc,) = product(
                [(n - 1, False, held[:2]), (1 - n, True, held[2:])], staged, acc, None, features, f"mm{n - 1}"
            )
            next_a, acc = tie(next_a, acc)
        held = [a, b, from_a, from_b]
        a, b = next_a, next_b
    (acc,) = product(
        [(half - 1, False, held[:2]), (1 - half, True, held[2:])], staged, acc, None, features, f"mm{half - 1}"
    )
    a, acc = tie(a, acc)
    keys, values = product([(half, False, [a, swap(a)])], staged, acc, sums, features, "mm_last")
    return new_base, new_mom, keys, values


def solution(mesh):
    placed = (
        P(("replica", "fsdp"), None),
        P(),
        P(None, "fsdp", "tensor"),
        P(None, "fsdp", "tensor"),
        P("replica", None, "fsdp", "tensor"),
    )
    return jax.shard_map(
        on_device,
        mesh=mesh,
        in_specs=placed,
        out_specs=(
            P(None, ("fsdp", "replica"), "tensor"),
            P(None, ("fsdp", "replica"), "tensor"),
            P(("replica", "fsdp"), "tensor"),
            P(("replica", "fsdp"), "tensor"),
        ),
        check_vma=False,
    )
```
